128 devices in a mesh: path: 16 (over x, z), fsdp: 8 (over y, core).
Axes of the slice: x: 4, y: 4, z: 4, core: 2. Of those that a mesh axis runs over, the one named last changes fastest.
Arguments:
- tokens: bfloat16 [16, 1024, 2048], P('path', 'fsdp'), may hold values from -6 to 6
- cotangent: bfloat16 [16, 1024, 2048], P('path', 'fsdp'), may hold values from -6 to 6
- norm_gain: float32 [16, 2, 2048], P('path'), may hold values from 0.1 to 1.9
- up_proj: bfloat16 [16, 2, 2048, 4096], P('path', None, None, 'fsdp'), as said below
- down_proj: bfloat16 [16, 2, 2048, 4096], P('path', None, None, 'fsdp'), as said below
- mom_up: float32 [8, 2048, 4096], P(None, 'path', 'fsdp'), may hold values from -4 to 4
- mom_down: float32 [8, 2048, 4096], P(None, 'path', 'fsdp'), may hold values from -4 to 4
- share_table: int32 [16, 2], replicated, may hold values from 0 to 3, as said below
- module_slot: int32 [8], replicated, may hold values from 0 to 7, each once
Outputs:
- new_up: bfloat16 [16, 2, 2048, 4096], P('path', None, None, 'fsdp')
- new_down: bfloat16 [16, 2, 2048, 4096], P('path', None, None, 'fsdp')
- new_mom_up: float32 [8, 2048, 4096], P(None, 'path', 'fsdp')
- new_mom_down: float32 [8, 2048, 4096], P(None, 'path', 'fsdp')
The draws below stay inside these ranges and needn't reach their ends.
Inputs may be any that keep to these rules, and one draw needn't show every extreme that they name: share_table[p, l] is the index, within level l, of the module that path p uses; a module may be shared by several paths or by none. Copies of one module are equal: up_proj[p, l] equals up_proj[q, l] and down_proj[p, l] equals down_proj[q, l] whenever share_table[p, l] = share_table[q, l]. `down_proj`: copies of one module are equal, as for up_proj.
All inputs are finite; a program needn't handle non-finite values.
Results may differ from the reference program's by a relative error of at most 0.012.
Values may be sent and summed in bfloat16 or wider, within the bound.
A program may use at most 128 MiB of HBM per device.

```python
import math
import jax
import jax.numpy as jnp
from jax import lax

D = 2048
FF = 4096
LEVELS = 2
PER_LEVEL = 4
SEQ_TOK = 1024
MODULES = 8
N_PATH = 16
N_FSDP = 8


def table_draw(key):
    first_key, second_key, order_key = jax.random.split(key, 3)
    left_pick = jax.random.randint(first_key, (N_PATH, LEVELS), 0, PER_LEVEL)
    right_pick = jax.random.randint(second_key, (N_PATH, LEVELS), 0, PER_LEVEL)
    smaller = jnp.minimum(left_pick, right_pick)
    orders = jnp.stack([jax.random.permutation(jax.random.fold_in(order_key, level_index), PER_LEVEL) for level_index in range(LEVELS)], axis=0)
    picked = jnp.take_along_axis(orders, smaller.T, axis=1).T.astype(jnp.int32)
    row_ids = jnp.arange(N_PATH, dtype=jnp.int32)
    columns = []
    for level_index in range(LEVELS):
        chosen = jax.random.permutation(jax.random.fold_in(key, 97 + level_index), N_PATH).astype(jnp.int32)
        column = picked[:, level_index]
        column = jnp.where(row_ids == chosen[0], PER_LEVEL - 1, column)
        column = jnp.where(row_ids == chosen[1], 0, column)
        columns.append(column)
    return jnp.stack(columns, axis=1).astype(jnp.int32)


def module_copies(key, salt):
    table = table_draw(jax.random.fold_in(key, 11))
    pool = jax.random.normal(jax.random.fold_in(key, salt), (LEVELS * PER_LEVEL, D, FF), jnp.float32)
    module_ids = jnp.arange(LEVELS, dtype=jnp.int32)[None, :] * PER_LEVEL + table
    return pool[module_ids].astype(jnp.bfloat16)


def draw_share_table(key, part):
    return table_draw(jax.random.fold_in(key, 11))


def draw_up_proj(key, part):
    return module_copies(key, 31)


def draw_down_proj(key, part):
    return module_copies(key, 41)


def levels(key, shape, shards, smallest, high):
    def one(axis_at, shards_of):
        heights = jax.random.uniform(jax.random.fold_in(jax.random.fold_in(key, 6), axis_at), (shards_of,), jnp.float32, smallest / len(shards), high / len(shards))
        return jnp.repeat(jnp.exp(heights), shape[axis_at] // shards_of).reshape((-1,) + (1,) * (len(shape) - axis_at - 1))

    level = one(*shards[0])
    for cut in shards[1:]:
        level = level * one(*cut)
    return level


def gaussian(own_key, dims, spread, bound, cuts=(), kind=jnp.bfloat16):
    entries = jax.random.normal(own_key, dims, jnp.float32) * spread
    if len(cuts) > 0:
        entries = levels(own_key, dims, cuts, -0.22, 0.18) * entries
    return jnp.clip(entries, min=-bound, max=bound).astype(kind)


def setup_inputs(seed: int = 0) -> dict:
    streams_of = jax.random.split(jax.random.key(seed), 10)
    return {
        "tokens": gaussian(streams_of[0], (N_PATH, SEQ_TOK, D), 1.0, 6.0, ((0, 16), (1, 8))),
        "cotangent": gaussian(streams_of[1], (N_PATH, SEQ_TOK, D), 1.0, 6.0, ((0, 16), (1, 8))),
        "norm_gain": jnp.clip(1.0 + 0.18 * jax.random.normal(streams_of[2], (N_PATH, LEVELS, D), jnp.float32), 0.1, 1.9),
        "up_proj": draw_up_proj(jax.random.fold_in(streams_of[9], 71), 0),
        "down_proj": draw_down_proj(jax.random.fold_in(streams_of[9], 71), 0),
        "mom_up": gaussian(streams_of[5], (MODULES, D, FF), 0.3, 4.0, ((1, 16), (2, 8)), jnp.float32),
        "mom_down": gaussian(streams_of[6], (MODULES, D, FF), 0.3, 4.0, ((1, 16), (2, 8)), jnp.float32),
        "share_table": draw_share_table(jax.random.fold_in(streams_of[9], 71), 0),
        "module_slot": jax.random.permutation(streams_of[8], MODULES).astype(jnp.int32),
    }


epsilon = 1e-06
gelu_coef = 0.7978845608
cubic_coef = 0.044715
momentum_decay = 0.9
outer_rate = 0.7

def gelu_tanh(value):
    inner = gelu_coef * (value + cubic_coef * value * value * value)
    return 0.5 * value * (1.0 + jnp.tanh(inner))

def gelu_slope(value):
    inner = gelu_coef * (value + cubic_coef * value * value * value)
    tangent = jnp.tanh(inner)
    return 0.5 * (1.0 + tangent) + 0.5 * value * (1.0 - tangent * tangent) * gelu_coef * (1.0 + 3.0 * cubic_coef * value * value)

def rms_norm(rows, gain):
    return rows * lax.rsqrt(lax.optimization_barrier(jnp.mean(rows * rows, axis=-1, keepdims=True)) + epsilon) * gain

def norm_back(rows, gain, upstream):
    _, pull = jax.vjp(lambda inner_rows: rms_norm(inner_rows, gain), rows)
    return pull(upstream)[0]

def contract_last(left, right):
    return lax.dot_general(left, right, (((1,), (1,)), ((), ())), preferred_element_type=jnp.float32)

def contract_first(left, right):
    return lax.dot_general(left, right, (((0,), (0,)), ((), ())), preferred_element_type=jnp.float32)

def block_sum(left, right, factor):
    width = left.shape[1] // N_FSDP
    summed = jnp.zeros((left.shape[0], right.shape[0]), jnp.float32)
    for block in range(N_FSDP):
        part = contract_last(left[:, block * width:(block + 1) * width], right[:, block * width:(block + 1) * width]) * factor
        rounded = lax.optimization_barrier(part.astype(jnp.bfloat16)).astype(jnp.float32)
        summed = summed + rounded
    return summed

def path_deltas(items):
    tok, cot, gain_pair, ups, downs = items
    scale_in = 1.0 / math.sqrt(D)
    scale_out = 1.0 / math.sqrt(FF)
    tok_float = tok.astype(jnp.float32)
    cot_float = cot.astype(jnp.float32)
    first_normed = rms_norm(tok_float, gain_pair[0]).astype(jnp.bfloat16)
    first_pre = jnp.dot(first_normed, ups[0], preferred_element_type=jnp.float32) * scale_in
    first_hidden = gelu_tanh(first_pre).astype(jnp.bfloat16)
    second_input = tok_float + block_sum(first_hidden, downs[0], scale_out)
    second_normed = rms_norm(second_input, gain_pair[1]).astype(jnp.bfloat16)
    second_pre = jnp.dot(second_normed, ups[1], preferred_element_type=jnp.float32) * scale_in
    second_hidden = gelu_tanh(second_pre).astype(jnp.bfloat16)
    grad_down_upper = contract_first(cot, second_hidden) * scale_out
    second_slope = (jnp.dot(cot, downs[1], preferred_element_type=jnp.float32) * scale_out * gelu_slope(second_pre)).astype(jnp.bfloat16)
    grad_up_upper = contract_first(second_normed, second_slope) * scale_in
    second_back = block_sum(second_slope, ups[1], scale_in)
    first_grad = (cot_float + norm_back(second_input, gain_pair[1], second_back)).astype(jnp.bfloat16)
    grad_down_lower = contract_first(first_grad, first_hidden) * scale_out
    first_slope = (jnp.dot(first_grad, downs[0], preferred_element_type=jnp.float32) * scale_out * gelu_slope(first_pre)).astype(jnp.bfloat16)
    grad_up_lower = contract_first(first_normed, first_slope) * scale_in
    lower_pair = jnp.stack([grad_up_lower, grad_down_lower])
    upper_pair = jnp.stack([grad_up_upper, grad_down_upper])
    return jnp.stack([lower_pair, upper_pair]).astype(jnp.bfloat16)

def reference(tokens, cotangent, norm_gain, up_proj, down_proj, mom_up, mom_down, share_table, module_slot):
    deltas = lax.map(path_deltas, (tokens, cotangent, norm_gain, up_proj, down_proj))
    module_ids = jnp.arange(LEVELS, dtype=jnp.int32)[None, :] * PER_LEVEL + share_table
    slot_of = module_slot[module_ids].astype(jnp.int32)
    flat_slots = slot_of.reshape(-1)
    flat_deltas = deltas.reshape(N_PATH * LEVELS, 2, D, FF)

    def accumulate(index, summed):
        return summed.at[flat_slots[index]].add(flat_deltas[index].astype(jnp.float32))
    summed = lax.fori_loop(0, N_PATH * LEVELS, accumulate, jnp.zeros((MODULES, 2, D, FF), jnp.float32))
    counts = lax.optimization_barrier(jnp.sum((flat_slots[None, :] == jnp.arange(MODULES, dtype=jnp.int32)[:, None]).astype(jnp.float32), axis=1))
    pseudo = summed / jnp.maximum(counts, 1.0)[:, None, None, None]
    new_mom_up = momentum_decay * mom_up + pseudo[:, 0]
    new_mom_down = momentum_decay * mom_down + pseudo[:, 1]
    outer_step = (pseudo + momentum_decay * jnp.stack([new_mom_up, new_mom_down], axis=1)).astype(jnp.bfloat16)
    routed = outer_step[slot_of]
    new_up = (up_proj.astype(jnp.float32) - outer_rate * routed[:, :, 0].astype(jnp.float32)).astype(jnp.bfloat16)
    new_down = (down_proj.astype(jnp.float32) - outer_rate * routed[:, :, 1].astype(jnp.float32)).astype(jnp.bfloat16)
    return (new_up, new_down, new_mom_up, new_mom_down)
```

```python
import functools
import math

import jax
import jax.numpy as jnp
from jax import lax
from jax.experimental import pallas as pl
from jax.experimental.pallas import tpu as pltpu
from jax.sharding import PartitionSpec as P

PER_LEVEL = 4

epsilon = 1e-06
gelu_coef = 0.7978845608
cubic_coef = 0.044715
momentum_decay = 0.9
outer_rate = 0.7


def gelu_tanh(value):
    inner = gelu_coef * (value + cubic_coef * value * value * value)
    return 0.5 * value * (1.0 + jnp.tanh(inner))


def gelu_slope(value):
    inner = gelu_coef * (value + cubic_coef * value * value * value)
    tangent = jnp.tanh(inner)
    return 0.5 * (1.0 + tangent) + 0.5 * value * (1.0 - tangent * tangent) * gelu_coef * (
        1.0 + 3.0 * cubic_coef * value * value
    )


def rms_norm(rows, gain):
    return rows * lax.rsqrt(jnp.mean(rows * rows, axis=-1, keepdims=True) + epsilon) * gain


def norm_back(rows, gain, upstream):
    _, pull = jax.vjp(lambda inner_rows: rms_norm(inner_rows, gain), rows)
    return pull(upstream)[0]


def contract_last(left, right):
    return lax.dot_general(
        left, right, (((1,), (1,)), ((), ())), preferred_element_type=jnp.float32
    )


def contract_first(left, right):
    return lax.dot_general(
        left, right, (((0,), (0,)), ((), ())), preferred_element_type=jnp.float32
    )


def combine_body(level, paths, share_ref, slot_ref, *refs):
    recv_up, recv_down, mom_up, mom_down = refs[:4]
    out_up, out_down, send_up, send_down, acc_up, acc_down = refs[-6:]
    module = pl.program_id(1)
    acc_up[...] = jnp.zeros_like(acc_up)
    acc_down[...] = jnp.zeros_like(acc_down)
    count = jnp.float32(0.0)
    for path in range(paths):
        hit = share_ref[path, level] == module
        count = count + jnp.where(hit, 1.0, 0.0)

        @pl.when(hit)
        def _():
            acc_up[...] += recv_up[path].astype(jnp.float32)
            acc_down[...] += recv_down[path].astype(jnp.float32)

    inverse = 1.0 / jnp.full((1, acc_up.shape[1]), jnp.maximum(count, 1.0), jnp.float32)
    for acc, mom, out in ((acc_up, mom_up, out_up), (acc_down, mom_down, out_down)):
        pseudo = acc[...] * inverse
        fresh = momentum_decay * mom[0] + pseudo
        out[0] = fresh
        acc[...] = pseudo + momentum_decay * fresh
    for path in range(paths):

        @pl.when(share_ref[path, level] == module)
        def _():
            send_up[path] = acc_up[...].astype(jnp.bfloat16)
            send_down[path] = acc_down[...].astype(jnp.bfloat16)


def combine(level, share, slots, recv_up, recv_down, mom_up, mom_down, partial):
    paths, rows, cols = recv_up.shape
    step = 32
    mom_spec = pl.BlockSpec(
        (1, step, cols), lambda r, m, share, slots: (slots[level * PER_LEVEL + m], r, 0)
    )
    path_spec = pl.BlockSpec((paths, step, cols), lambda r, m, share, slots: (0, r, 0))
    hold = [pl.BlockSpec(memory_space=pl.ANY)] * len(partial)
    return pl.pallas_call(
        functools.partial(combine_body, level, paths),
        grid_spec=pltpu.PrefetchScalarGridSpec(
            num_scalar_prefetch=2,
            grid=(rows // step, PER_LEVEL),
            in_specs=[path_spec, path_spec, mom_spec, mom_spec] + hold,
            out_specs=[mom_spec, mom_spec, path_spec, path_spec],
            scratch_shapes=[pltpu.VMEM((step, cols), jnp.float32)] * 2,
        ),
        out_shape=[
            jax.ShapeDtypeStruct(mom_up.shape, jnp.float32),
            jax.ShapeDtypeStruct(mom_up.shape, jnp.float32),
            jax.ShapeDtypeStruct(recv_up.shape, jnp.bfloat16),
            jax.ShapeDtypeStruct(recv_up.shape, jnp.bfloat16),
        ],
        input_output_aliases={6: 0, 7: 1} if partial else {},
        cost_estimate=pl.CostEstimate(
            flops=8 * recv_up.size, bytes_accessed=16 * recv_up.size, transcendentals=0
        ),
        name="combine",
    )(share, slots, recv_up, recv_down, mom_up, mom_down, *partial)


def update_body(up_ref, down_ref, back_up, back_down, *refs):
    new_up, new_down = refs[-2:]
    for old, back, new in ((up_ref, back_up, new_up), (down_ref, back_down, new_down)):
        new[0, 0] = (
            old[0, 0].astype(jnp.float32) - outer_rate * back[...].astype(jnp.float32)
        ).astype(jnp.bfloat16)


def update(level, up, down, back_up, back_down, partial):
    _, _, rows, cols = up.shape
    step = 512
    full = pl.BlockSpec((1, 1, step, cols), lambda r: (0, level, r, 0))
    flat = pl.BlockSpec((step, cols), lambda r: (r, 0))
    hold = [pl.BlockSpec(memory_space=pl.ANY)] * len(partial)
    return pl.pallas_call(
        update_body,
        grid=(rows // step,),
        in_specs=[full, full, flat, flat] + hold,
        out_specs=[full, full],
        out_shape=[jax.ShapeDtypeStruct(up.shape, up.dtype)] * 2,
        input_output_aliases={4: 0, 5: 1} if partial else {},
        cost_estimate=pl.CostEstimate(
            flops=4 * rows * cols, bytes_accessed=12 * rows * cols, transcendentals=0
        ),
        name="update",
    )(up, down, back_up.reshape(rows, cols), back_down.reshape(rows, cols), *partial)


def swap(value):
    return lax.all_to_all(value, "path", split_axis=0, concat_axis=0, tiled=True)


def shards(
    tokens, cotangent, norm_gain, up_proj, down_proj, mom_up, mom_down, share_table, module_slot
):
    scale_in = 1.0 / math.sqrt(2048)
    scale_out = 1.0 / math.sqrt(4096)
    norm_gains = norm_gain[0]
    up_local = up_proj[0]
    down_local = down_proj[0]
    paths = share_table.shape[0]
    row_block, col_block = mom_up.shape[1:]

    def blocks(grad):
        return grad.astype(jnp.bfloat16).reshape(paths, row_block, col_block)

    def exchange(level, grad_up, grad_down, partial):
        recv_up, recv_down = swap(blocks(grad_up)), swap(blocks(grad_down))
        return combine(
            level, share_table, module_slot, recv_up, recv_down, mom_up, mom_down, partial
        )

    tok_all, cot_all = (
        lax.all_gather(tokens[0], "fsdp", axis=0, tiled=True),
        lax.all_gather(cotangent[0], "fsdp", axis=0, tiled=True),
    )
    tok_float = tok_all.astype(jnp.float32)
    first_normed = rms_norm(tok_float, norm_gains[0]).astype(jnp.bfloat16)
    first_pre = jnp.dot(first_normed, up_local[0], preferred_element_type=jnp.float32) * scale_in
    first_hidden = gelu_tanh(first_pre).astype(jnp.bfloat16)
    hidden_summed = lax.psum(
        (contract_last(first_hidden, down_local[0]) * scale_out).astype(jnp.bfloat16), "fsdp"
    ).astype(jnp.float32)
    second_input = tok_float + hidden_summed
    second_normed = rms_norm(second_input, norm_gains[1]).astype(jnp.bfloat16)
    second_pre = jnp.dot(second_normed, up_local[1], preferred_element_type=jnp.float32) * scale_in
    second_hidden = gelu_tanh(second_pre).astype(jnp.bfloat16)
    grad_down_upper = contract_first(cot_all, second_hidden) * scale_out
    second_slope = (
        jnp.dot(cot_all, down_local[1], preferred_element_type=jnp.float32)
        * scale_out
        * gelu_slope(second_pre)
    ).astype(jnp.bfloat16)
    grad_up_upper = contract_first(second_normed, second_slope) * scale_in
    mom_up_1, mom_down_1, send_up_1, send_down_1 = exchange(1, grad_up_upper, grad_down_upper, ())
    back_summed = lax.psum(
        (contract_last(second_slope, up_local[1]) * scale_in).astype(jnp.bfloat16), "fsdp"
    ).astype(jnp.float32)
    first_grad = (
        cot_all.astype(jnp.float32) + norm_back(second_input, norm_gains[1], back_summed)
    ).astype(jnp.bfloat16)
    grad_down_lower = contract_first(first_grad, first_hidden) * scale_out
    first_slope = (
        jnp.dot(first_grad, down_local[0], preferred_element_type=jnp.float32)
        * scale_out
        * gelu_slope(first_pre)
    ).astype(jnp.bfloat16)
    grad_up_lower = contract_first(first_normed, first_slope) * scale_in
    new_mom_up, new_mom_down, send_up_0, send_down_0 = exchange(
        0, grad_up_lower, grad_down_lower, (mom_up_1, mom_down_1)
    )
    partial = update(1, up_proj, down_proj, swap(send_up_1), swap(send_down_1), ())
    new_up, new_down = update(0, up_proj, down_proj, swap(send_up_0), swap(send_down_0), partial)
    return (new_up, new_down, new_mom_up, new_mom_down)


def solution(mesh):
    in_specs = (
        P("path", "fsdp", None),
        P("path", "fsdp", None),
        P("path", None, None),
        P("path", None, None, "fsdp"),
        P("path", None, None, "fsdp"),
        P(None, "path", "fsdp"),
        P(None, "path", "fsdp"),
        P(),
        P(),
    )
    out_specs = (
        P("path", None, None, "fsdp"),
        P("path", None, None, "fsdp"),
        P(None, "path", "fsdp"),
        P(None, "path", "fsdp"),
    )
    return jax.shard_map(shards, mesh=mesh, in_specs=in_specs, out_specs=out_specs, check_vma=False)
```

```python
import functools
import math

import jax
import jax.numpy as jnp
from jax import lax
from jax.experimental import pallas as pl
from jax.experimental.pallas import tpu as pltpu
from jax.sharding import PartitionSpec as P

PER_LEVEL = 4

epsilon = 1e-06
gelu_coef = 0.7978845608
cubic_coef = 0.044715
momentum_decay = 0.9
outer_rate = 0.7


def gelu_tanh(value):
    inner = gelu_coef * (value + cubic_coef * value * value * value)
    return 0.5 * value * (1.0 + jnp.tanh(inner))


def gelu_slope(value):
    inner = gelu_coef * (value + cubic_coef * value * value * value)
    tangent = jnp.tanh(inner)
    return 0.5 * (1.0 + tangent) + 0.5 * value * (1.0 - tangent * tangent) * gelu_coef * (
        1.0 + 3.0 * cubic_coef * value * value
    )


def rms_norm(rows, gain):
    return rows * lax.rsqrt(jnp.mean(rows * rows, axis=-1, keepdims=True) + epsilon) * gain


def norm_back(rows, gain, upstream):
    _, pull = jax.vjp(lambda inner_rows: rms_norm(inner_rows, gain), rows)
    return pull(upstream)[0]


def contract_last(left, right):
    return lax.dot_general(
        left, right, (((1,), (1,)), ((), ())), preferred_element_type=jnp.float32
    )


def contract_first(left, right):
    return lax.dot_general(
        left, right, (((0,), (0,)), ((), ())), preferred_element_type=jnp.float32
    )


def combine_body(level, paths, share_ref, slot_ref, recv, mom, *refs):
    out, send, acc = refs[-3:]
    module = pl.program_id(1)
    acc[...] = jnp.zeros_like(acc)
    count = jnp.float32(0.0)
    for path in range(paths):
        hit = share_ref[path, level] == module
        count = count + jnp.where(hit, 1.0, 0.0)

        @pl.when(hit)
        def _():
            acc[...] += recv[path].astype(jnp.float32)

    divisor = jnp.full((1, acc.shape[1]), jnp.maximum(count, 1.0), jnp.float32)
    pseudo = acc[...] * (1.0 / divisor)
    fresh = momentum_decay * mom[0] + pseudo
    out[0] = fresh
    acc[...] = pseudo + momentum_decay * fresh
    for path in range(paths):

        @pl.when(share_ref[path, level] == module)
        def _():
            send[path] = acc[...].astype(jnp.bfloat16)


def combine(level, share, slots, recv, mom, partial):
    paths, rows, cols = recv.shape
    step = 32
    mom_spec = pl.BlockSpec(
        (1, step, cols), lambda r, m, share, slots: (slots[level * PER_LEVEL + m], r, 0)
    )
    path_spec = pl.BlockSpec((paths, step, cols), lambda r, m, share, slots: (0, r, 0))
    hold = [pl.BlockSpec(memory_space=pl.ANY)] * len(partial)
    return pl.pallas_call(
        functools.partial(combine_body, level, paths),
        grid_spec=pltpu.PrefetchScalarGridSpec(
            num_scalar_prefetch=2,
            grid=(rows // step, PER_LEVEL),
            in_specs=[path_spec, mom_spec] + hold,
            out_specs=[mom_spec, path_spec],
            scratch_shapes=[pltpu.VMEM((step, cols), jnp.float32)],
        ),
        out_shape=[
            jax.ShapeDtypeStruct(mom.shape, jnp.float32),
            jax.ShapeDtypeStruct(recv.shape, jnp.bfloat16),
        ],
        input_output_aliases={4: 0} if partial else {},
        cost_estimate=pl.CostEstimate(
            flops=4 * recv.size, bytes_accessed=8 * recv.size, transcendentals=0
        ),
        name="combine",
    )(share, slots, recv, mom, *partial)


def update_body(old, back, *refs):
    new = refs[-1]
    new[0, 0] = (
        old[0, 0].astype(jnp.float32) - outer_rate * back[...].astype(jnp.float32)
    ).astype(jnp.bfloat16)


def update(level, proj, back, partial):
    _, _, rows, cols = proj.shape
    step = 512
    full = pl.BlockSpec((1, 1, step, cols), lambda r: (0, level, r, 0))
    flat = pl.BlockSpec((step, cols), lambda r: (r, 0))
    hold = [pl.BlockSpec(memory_space=pl.ANY)] * len(partial)
    return pl.pallas_call(
        update_body,
        grid=(rows // step,),
        in_specs=[full, flat] + hold,
        out_specs=full,
        out_shape=jax.ShapeDtypeStruct(proj.shape, proj.dtype),
        input_output_aliases={2: 0} if partial else {},
        cost_estimate=pl.CostEstimate(
            flops=2 * rows * cols, bytes_accessed=6 * rows * cols, transcendentals=0
        ),
        name="update",
    )(proj, back.reshape(rows, cols), *partial)


def cube():
    place = lax.axis_index("fsdp")
    row, core = place // 2, place % 2
    across = row + 1 - 2 * (row % 2)
    return row, core, across, 3 - row, (row + 2) % 4


def greet(peers):
    barrier = pltpu.get_barrier_semaphore()
    for peer in peers:
        pl.semaphore_signal(
            barrier, inc=1, device_id={"fsdp": peer}, device_id_type=pl.DeviceIdType.MESH
        )
    pl.semaphore_wait(barrier, len(peers))


def gather_body(own, out, send_sem, recv_sem, local_sem):
    row, core, row_a, row_b, row_d = cube()
    me, sibling = row * 2 + core, row * 2 + 1 - core
    peer_a, peer_b, block_d = row_a * 2 + core, row_b * 2 + core, row_d * 2 + core
    greet((sibling, peer_a, peer_b))
    half = own.shape[0] // 2
    parts = (pl.ds(0, half), pl.ds(half, half))

    def copy(index, source, block, part, peer):
        return pltpu.make_async_remote_copy(
            src_ref=source,
            dst_ref=out.at[block, part],
            send_sem=send_sem.at[index],
            recv_sem=recv_sem.at[index],
            device_id={"fsdp": peer},
            device_id_type=pl.DeviceIdType.MESH,
        )

    whole = pl.ds(0, own.shape[0])
    first, second = parts
    a_second = copy(0, own.at[second], me, second, peer_a)
    b_first = copy(1, own.at[first], me, first, peer_b)
    a_first = copy(2, own.at[first], me, first, peer_a)
    b_second = copy(3, own.at[second], me, second, peer_b)
    mine = copy(4, own, me, whole, sibling)
    stay = pltpu.make_async_copy(own, out.at[me], local_sem)
    for step in (a_second, b_first, a_first, b_second, mine, stay):
        step.start()

    def relay(index, block, part, peer):
        return copy(index, out.at[block, part], block, part, peer)

    b_first.wait_recv()
    onward_a = relay(5, peer_b, first, peer_a)
    onward_a.start()
    a_second.wait_recv()
    onward_b = relay(6, peer_a, second, peer_b)
    onward_b.start()
    side = [relay(7, peer_b, first, sibling), relay(8, peer_a, second, sibling)]
    for step in side:
        step.start()
    a_first.wait_recv()
    side.append(relay(9, peer_a, first, sibling))
    side[-1].start()
    b_second.wait_recv()
    side.append(relay(10, peer_b, second, sibling))
    side[-1].start()
    onward_a.wait_recv()
    side.append(relay(11, block_d, first, sibling))
    side[-1].start()
    onward_b.wait_recv()
    side.append(relay(12, block_d, second, sibling))
    side[-1].start()
    mine.wait_recv()
    for step in side:
        step.wait_recv()
    stay.wait()
    for step in (a_second, b_first, a_first, b_second, mine, onward_a, onward_b, *side):
        step.wait_send()


def gather(own, collective):
    rows, cols = own.shape
    return pl.pallas_call(
        gather_body,
        in_specs=[pl.BlockSpec(memory_space=pltpu.VMEM)],
        out_specs=pl.BlockSpec(memory_space=pl.ANY),
        out_shape=jax.ShapeDtypeStruct((8, rows, cols), own.dtype),
        scratch_shapes=[
            pltpu.SemaphoreType.DMA((13,)),
            pltpu.SemaphoreType.DMA((13,)),
            pltpu.SemaphoreType.DMA,
        ],
        compiler_params=pltpu.CompilerParams(collective_id=collective, has_side_effects=True),
        cost_estimate=pl.CostEstimate(flops=0, bytes_accessed=60 * 2**20, transcendentals=0),
        name="gather",
    )(own).reshape(8 * rows, cols)


def scatter_body(parts_ref, out, near, summed, first_in, second_in, send_sem, recv_sem):
    row, core, row_a, row_b, row_d = cube()
    sibling = row * 2 + 1 - core
    peer_a, peer_b = row_a * 2 + core, row_b * 2 + core
    greet((sibling, peer_a, peer_b))
    half = out.shape[0] // 2
    top, low = pl.ds(0, half), pl.ds(half, half)
    order = (row_d, row_a, row_b, row)

    def copy(index, source, target, peer):
        return pltpu.make_async_remote_copy(
            src_ref=source,
            dst_ref=target,
            send_sem=send_sem.at[index],
            recv_sem=recv_sem.at[index],
            device_id={"fsdp": peer},
            device_id_type=pl.DeviceIdType.MESH,
        )

    swaps = [
        copy(k, parts_ref.at[order[k] * 2 + 1 - core], near.at[k], sibling) for k in range(4)
    ]
    for step in swaps:
        step.start()

    def settle(k):
        swaps[k].wait_recv()
        mine = parts_ref[order[k] * 2 + core].astype(jnp.float32)
        summed[k] = (mine + near[k].astype(jnp.float32)).astype(jnp.bfloat16)

    settle(0)
    settle(1)
    far_a = copy(4, summed.at[0, top], first_in.at[0], peer_a)
    far_b = copy(5, summed.at[0, low], first_in.at[1], peer_b)
    far_a.start()
    far_b.start()
    settle(2)
    near_a = copy(6, summed.at[1, top], first_in.at[2], peer_a)
    near_a.start()
    settle(3)
    near_b = copy(7, summed.at[2, low], first_in.at[3], peer_b)
    near_b.start()
    far_a.wait_recv()
    second_in[0] = (
        summed[2, top].astype(jnp.float32) + first_in[0].astype(jnp.float32)
    ).astype(jnp.bfloat16)
    far_b.wait_recv()
    second_in[1] = (
        summed[1, low].astype(jnp.float32) + first_in[1].astype(jnp.float32)
    ).astype(jnp.bfloat16)
    last_b = copy(8, second_in.at[0], second_in.at[2], peer_b)
    last_b.start()
    near_a.wait_recv()
    out[top] = summed[3, top].astype(jnp.float32) + first_in[2].astype(jnp.float32)
    last_a = copy(9, second_in.at[1], second_in.at[3], peer_a)
    last_a.start()
    near_b.wait_recv()
    out[low] = summed[3, low].astype(jnp.float32) + first_in[3].astype(jnp.float32)
    last_b.wait_recv()
    out[top] += second_in[2].astype(jnp.float32)
    last_a.wait_recv()
    out[low] += second_in[3].astype(jnp.float32)
    for step in (*swaps, far_a, far_b, near_a, near_b, last_a, last_b):
        step.wait_send()


def scatter(parts, collective):
    rows, cols = parts.shape
    rows = rows // 8
    return pl.pallas_call(
        scatter_body,
        in_specs=[pl.BlockSpec(memory_space=pltpu.VMEM)],
        out_specs=pl.BlockSpec(memory_space=pltpu.VMEM),
        out_shape=jax.ShapeDtypeStruct((rows, cols), jnp.float32),
        scratch_shapes=[
            pltpu.VMEM((4, rows, cols), jnp.bfloat16),
            pltpu.VMEM((4, rows, cols), jnp.bfloat16),
            pltpu.VMEM((4, rows // 2, cols), jnp.bfloat16),
            pltpu.VMEM((4, rows // 2, cols), jnp.bfloat16),
            pltpu.SemaphoreType.DMA((10,)),
            pltpu.SemaphoreType.DMA((10,)),
        ],
        compiler_params=pltpu.CompilerParams(collective_id=collective, has_side_effects=True),
        cost_estimate=pl.CostEstimate(flops=0, bytes_accessed=70 * 2**20, transcendentals=0),
        name="scatter",
    )(parts.reshape(8, rows, cols))


def swap(value):
    return lax.all_to_all(value, "path", split_axis=0, concat_axis=0, tiled=True)


def shards(
    tokens, cotangent, norm_gain, up_proj, down_proj, mom_up, mom_down, share_table, module_slot
):
    scale_in = 1.0 / math.sqrt(2048)
    scale_out = 1.0 / math.sqrt(4096)
    norm_gains = norm_gain[0]
    up_local = up_proj[0]
    down_local = down_proj[0]
    paths = share_table.shape[0]
    row_block, col_block = mom_up.shape[1:]

    def blocks(grad):
        return grad.astype(jnp.bfloat16).reshape(paths, row_block, col_block)

    def merge(level, recv, mom, partial):
        return combine(level, share_table, module_slot, recv, mom, partial)

    tie = lax.optimization_barrier

    cot_all = lax.all_gather(cotangent[0], "fsdp", axis=0, tiled=True)
    tok_float = tokens[0].astype(jnp.float32)
    first_normed = gather(rms_norm(tok_float, norm_gains[0]).astype(jnp.bfloat16), 0)
    first_pre = jnp.dot(first_normed, up_local[0], preferred_element_type=jnp.float32) * scale_in
    first_hidden = gelu_tanh(first_pre).astype(jnp.bfloat16)
    second_input = tok_float + scatter(
        (contract_last(first_hidden, down_local[0]) * scale_out).astype(jnp.bfloat16), 1
    )
    second_normed = gather(rms_norm(second_input, norm_gains[1]).astype(jnp.bfloat16), 2)
    second_pre = jnp.dot(second_normed, up_local[1], preferred_element_type=jnp.float32) * scale_in
    second_hidden = gelu_tanh(second_pre).astype(jnp.bfloat16)
    grad_down_upper = contract_first(cot_all, second_hidden) * scale_out
    recv_down_1 = swap(blocks(grad_down_upper))
    second_slope = (
        jnp.dot(cot_all, down_local[1], preferred_element_type=jnp.float32)
        * scale_out
        * gelu_slope(second_pre)
    ).astype(jnp.bfloat16)
    grad_up_upper = contract_first(second_normed, second_slope) * scale_in
    back_parts = (contract_last(second_slope, up_local[1]) * scale_in).astype(jnp.bfloat16)
    grad_up_upper, recv_down_1, back_parts = tie(
        (blocks(grad_up_upper), recv_down_1, back_parts)
    )
    recv_up_1 = swap(grad_up_upper)
    back_summed = scatter(back_parts, 3)
    own_grad = (
        cotangent[0].astype(jnp.float32) + norm_back(second_input, norm_gains[1], back_summed)
    ).astype(jnp.bfloat16)
    mom_down_1, send_down_1 = merge(1, recv_down_1, mom_down, ())
    own_grad, send_down_1, recv_up_1 = tie((own_grad, send_down_1, recv_up_1))
    back_down_1 = swap(send_down_1)
    first_grad, back_down_1 = tie((gather(own_grad, 4), back_down_1))
    grad_down_lower = contract_first(first_grad, first_hidden) * scale_out
    first_slope = (
        jnp.dot(first_grad, down_local[0], preferred_element_type=jnp.float32)
        * scale_out
        * gelu_slope(first_pre)
    ).astype(jnp.bfloat16)
    grad_up_lower = contract_first(first_normed, first_slope) * scale_in
    mom_up_1, send_up_1 = merge(1, recv_up_1, mom_up, ())
    recv_down_0 = swap(blocks(grad_down_lower))
    grad_up_lower, recv_down_0 = tie((blocks(grad_up_lower), recv_down_0))
    recv_up_0 = swap(grad_up_lower)
    new_mom_down, send_down_0 = merge(0, recv_down_0, mom_down, (mom_down_1,))
    send_up_1, recv_up_0 = tie((send_up_1, recv_up_0))
    back_up_1 = swap(send_up_1)
    new_mom_up, send_up_0 = merge(0, recv_up_0, mom_up, (mom_up_1,))
    send_down_0, back_up_1 = tie((send_down_0, back_up_1))
    back_down_0 = swap(send_down_0)
    send_up_0, back_down_0 = tie((send_up_0, back_down_0))
    back_up_0 = swap(send_up_0)
    down_1 = update(1, down_proj, back_down_1, ())
    up_1 = update(1, up_proj, back_up_1, ())
    new_down = update(0, down_proj, back_down_0, (down_1,))
    new_up = update(0, up_proj, back_up_0, (up_1,))
    return (new_up, new_down, new_mom_up, new_mom_down)


def solution(mesh):
    in_specs = (
        P("path", "fsdp", None),
        P("path", "fsdp", None),
        P("path", None, None),
        P("path", None, None, "fsdp"),
        P("path", None, None, "fsdp"),
        P(None, "path", "fsdp"),
        P(None, "path", "fsdp"),
        P(),
        P(),
    )
    out_specs = (
        P("path", None, None, "fsdp"),
        P("path", None, None, "fsdp"),
        P(None, "path", "fsdp"),
        P(None, "path", "fsdp"),
    )
    return jax.shard_map(shards, mesh=mesh, in_specs=in_specs, out_specs=out_specs, check_vma=False)
```

```python
import functools
import math

import jax
import jax.numpy as jnp
from jax import lax
from jax.experimental import pallas as pl
from jax.experimental.pallas import tpu as pltpu
from jax.sharding import PartitionSpec as P

PER_LEVEL = 4

epsilon = 1e-06
gelu_coef = 0.7978845608
cubic_coef = 0.044715
momentum_decay = 0.9
outer_rate = 0.7


def gelu_tanh(value):
    inner = gelu_coef * (value + cubic_coef * value * value * value)
    return 0.5 * value * (1.0 + jnp.tanh(inner))


def gelu_slope(value):
    inner = gelu_coef * (value + cubic_coef * value * value * value)
    tangent = jnp.tanh(inner)
    return 0.5 * (1.0 + tangent) + 0.5 * value * (1.0 - tangent * tangent) * gelu_coef * (
        1.0 + 3.0 * cubic_coef * value * value
    )


def rms_norm(rows, gain):
    return rows * lax.rsqrt(jnp.mean(rows * rows, axis=-1, keepdims=True) + epsilon) * gain


def norm_back(rows, gain, upstream):
    _, pull = jax.vjp(lambda inner_rows: rms_norm(inner_rows, gain), rows)
    return pull(upstream)[0]


def contract_last(left, right):
    return lax.dot_general(
        left, right, (((1,), (1,)), ((), ())), preferred_element_type=jnp.float32
    )


def contract_first(left, right):
    return lax.dot_general(
        left, right, (((0,), (0,)), ((), ())), preferred_element_type=jnp.float32
    )


def place_body(slot_ref, fresh, *refs):
    refs[-1][...] = fresh[...]


def place(level, slots, fresh, slot_count, partial):
    _, rows, cols = fresh.shape
    hold = [pl.BlockSpec(memory_space=pl.ANY)] * len(partial)
    return pl.pallas_call(
        place_body,
        grid_spec=pltpu.PrefetchScalarGridSpec(
            num_scalar_prefetch=1,
            grid=(PER_LEVEL,),
            in_specs=[pl.BlockSpec((1, rows, cols), lambda m, slots: (m, 0, 0))] + hold,
            out_specs=pl.BlockSpec(
                (1, rows, cols), lambda m, slots: (slots[level * PER_LEVEL + m], 0, 0)
            ),
        ),
        out_shape=jax.ShapeDtypeStruct((slot_count, rows, cols), jnp.float32),
        input_output_aliases={2: 0} if partial else {},
        cost_estimate=pl.CostEstimate(
            flops=0, bytes_accessed=8 * fresh.size, transcendentals=0
        ),
        name="place",
    )(slots, fresh, *partial)


def update_body(old, back, *refs):
    new = refs[-1]
    new[0, 0] = (
        old[0, 0].astype(jnp.float32) - outer_rate * back[...].astype(jnp.float32)
    ).astype(jnp.bfloat16)


def update(level, proj, back, partial):
    _, _, rows, cols = proj.shape
    step = 512
    full = pl.BlockSpec((1, 1, step, cols), lambda r: (0, level, r, 0))
    flat = pl.BlockSpec((step, cols), lambda r: (r, 0))
    hold = [pl.BlockSpec(memory_space=pl.ANY)] * len(partial)
    return pl.pallas_call(
        update_body,
        grid=(rows // step,),
        in_specs=[full, flat] + hold,
        out_specs=full,
        out_shape=jax.ShapeDtypeStruct(proj.shape, proj.dtype),
        input_output_aliases={2: 0} if partial else {},
        cost_estimate=pl.CostEstimate(
            flops=2 * rows * cols, bytes_accessed=6 * rows * cols, transcendentals=0
        ),
        name="update",
    )(proj, back.reshape(rows, cols), *partial)


def cube():
    place = lax.axis_index("fsdp")
    row, core = place // 2, place % 2
    across = row + 1 - 2 * (row % 2)
    return row, core, across, 3 - row, (row + 2) % 4


def greet(peers):
    barrier = pltpu.get_barrier_semaphore()
    for peer in peers:
        pl.semaphore_signal(
            barrier, inc=1, device_id={"fsdp": peer}, device_id_type=pl.DeviceIdType.MESH
        )
    pl.semaphore_wait(barrier, len(peers))


class Spread:
    @staticmethod
    def scratch(rows, cols):
        sems = pltpu.SemaphoreType.DMA((13,))
        return [pltpu.VMEM((rows, cols), jnp.bfloat16), sems, sems, pltpu.SemaphoreType.DMA]

    def __init__(self, out, own, send_sem, recv_sem, local_sem):
        self.out, self.own = out, own
        self.send_sem, self.recv_sem, self.local_sem = send_sem, recv_sem, local_sem
        row, core, row_a, row_b, row_d = cube()
        self.me, self.sibling = row * 2 + core, row * 2 + 1 - core
        self.peer_a, self.peer_b = row_a * 2 + core, row_b * 2 + core
        self.block_d = row_d * 2 + core
        self.peers = (self.sibling, self.peer_a, self.peer_b)
        half = own.shape[0] // 2
        self.first, self.second = pl.ds(0, half), pl.ds(half, half)
        self.side, self.sent = [], []

    def copy(self, index, source, target, peer):
        copy = pltpu.make_async_remote_copy(
            src_ref=source,
            dst_ref=target,
            send_sem=self.send_sem.at[index],
            recv_sem=self.recv_sem.at[index],
            device_id={"fsdp": peer},
            device_id_type=pl.DeviceIdType.MESH,
        )
        copy.start()
        self.sent.append(copy)
        return copy

    def relay(self, index, block, part, peer):
        place = self.out.at[block, part]
        return self.copy(index, place, place, peer)

    def begin(self):
        own, out, me, first, second = self.own, self.out, self.me, self.first, self.second
        self.a_second = self.copy(0, own.at[second], out.at[me, second], self.peer_a)
        self.b_first = self.copy(1, own.at[first], out.at[me, first], self.peer_b)
        self.a_first = self.copy(2, own.at[first], out.at[me, first], self.peer_a)
        self.b_second = self.copy(3, own.at[second], out.at[me, second], self.peer_b)
        self.mine = self.copy(4, own, out.at[me], self.sibling)
        self.stay = pltpu.make_async_copy(own, out.at[me], self.local_sem)
        self.stay.start()

    def relay_first(self):
        self.b_first.wait_recv()
        self.onward_a = self.relay(5, self.peer_b, self.first, self.peer_a)
        self.a_second.wait_recv()
        self.onward_b = self.relay(6, self.peer_a, self.second, self.peer_b)
        self.side.append(self.relay(7, self.peer_b, self.first, self.sibling))
        self.side.append(self.relay(8, self.peer_a, self.second, self.sibling))

    def relay_second(self):
        self.a_first.wait_recv()
        self.side.append(self.relay(9, self.peer_a, self.first, self.sibling))
        self.b_second.wait_recv()
        self.side.append(self.relay(10, self.peer_b, self.second, self.sibling))

    def relay_last(self):
        self.onward_a.wait_recv()
        self.side.append(self.relay(11, self.block_d, self.first, self.sibling))
        self.onward_b.wait_recv()
        self.side.append(self.relay(12, self.block_d, self.second, self.sibling))

    def finish(self):
        self.mine.wait_recv()
        for copy in self.side:
            copy.wait_recv()
        self.stay.wait()
        for copy in self.sent:
            copy.wait_send()


def gather_body(own, out, *sems):
    spread = Spread(out, own, *sems)
    greet(spread.peers)
    spread.begin()
    spread.relay_first()
    spread.relay_second()
    spread.relay_last()
    spread.finish()


def gather(own, collective):
    rows, cols = own.shape
    return pl.pallas_call(
        gather_body,
        in_specs=[pl.BlockSpec(memory_space=pltpu.VMEM)],
        out_specs=pl.BlockSpec(memory_space=pl.ANY),
        out_shape=jax.ShapeDtypeStruct((8, rows, cols), own.dtype),
        scratch_shapes=Spread.scratch(rows, cols)[1:],
        compiler_params=pltpu.CompilerParams(collective_id=collective, has_side_effects=True),
        cost_estimate=pl.CostEstimate(flops=0, bytes_accessed=60 * 2**20, transcendentals=0),
        name="gather",
    )(own).reshape(8 * rows, cols)


class Scatter:
    @staticmethod
    def scratch(rows, cols):
        sems = pltpu.SemaphoreType.DMA((10,))
        pair = pltpu.VMEM((4, rows, cols), jnp.bfloat16)
        return [
            pair,
            pair,
            pltpu.VMEM((8, rows // 2, cols), jnp.bfloat16),
            pltpu.VMEM((rows, cols), jnp.float32),
            sems,
            sems,
        ]

    def __init__(self, parts_ref, near_in, summed, arrived, total, send_sem, recv_sem):
        self.parts, self.near_in, self.summed = parts_ref, near_in, summed
        self.arrived, self.total = arrived, total
        self.send_sem, self.recv_sem = send_sem, recv_sem
        row, self.core, row_a, row_b, row_d = cube()
        self.sibling = row * 2 + 1 - self.core
        self.peer_a, self.peer_b = row_a * 2 + self.core, row_b * 2 + self.core
        self.peers = (self.sibling, self.peer_a, self.peer_b)
        half = total.shape[0] // 2
        self.top, self.low = pl.ds(0, half), pl.ds(half, half)
        self.order = (row_d, row_a, row_b, row)
        self.sent = []

    def copy(self, index, source, target, peer):
        copy = pltpu.make_async_remote_copy(
            src_ref=source,
            dst_ref=target,
            send_sem=self.send_sem.at[index],
            recv_sem=self.recv_sem.at[index],
            device_id={"fsdp": peer},
            device_id_type=pl.DeviceIdType.MESH,
        )
        copy.start()
        self.sent.append(copy)
        return copy

    def begin(self):
        self.swaps = [
            self.copy(
                k,
                self.parts.at[self.order[k] * 2 + 1 - self.core],
                self.near_in.at[k],
                self.sibling,
            )
            for k in range(4)
        ]

    def settle(self, k):
        self.swaps[k].wait_recv()
        mine = self.parts[self.order[k] * 2 + self.core].astype(jnp.float32)
        self.summed[k] = (mine + self.near_in[k].astype(jnp.float32)).astype(jnp.bfloat16)

    def early(self):
        summed, arrived, top, low = self.summed, self.arrived, self.top, self.low
        self.settle(0)
        self.settle(1)
        self.far_a = self.copy(4, summed.at[0, top], arrived.at[0], self.peer_a)
        self.far_b = self.copy(5, summed.at[0, low], arrived.at[1], self.peer_b)
        self.settle(2)
        self.near_a = self.copy(6, summed.at[1, top], arrived.at[2], self.peer_a)
        self.settle(3)
        self.near_b = self.copy(7, summed.at[2, low], arrived.at[3], self.peer_b)

    def middle(self):
        summed, arrived = self.summed, self.arrived
        self.far_a.wait_recv()
        arrived[4] = (
            summed[2, self.top].astype(jnp.float32) + arrived[0].astype(jnp.float32)
        ).astype(jnp.bfloat16)
        self.far_b.wait_recv()
        arrived[5] = (
            summed[1, self.low].astype(jnp.float32) + arrived[1].astype(jnp.float32)
        ).astype(jnp.bfloat16)
        self.last_b = self.copy(8, arrived.at[4], arrived.at[6], self.peer_b)
        self.last_a = self.copy(9, arrived.at[5], arrived.at[7], self.peer_a)

    def near(self):
        summed, arrived = self.summed, self.arrived
        self.near_a.wait_recv()
        self.total[self.top] = summed[3, self.top].astype(jnp.float32) + arrived[2].astype(
            jnp.float32
        )
        self.near_b.wait_recv()
        self.total[self.low] = summed[3, self.low].astype(jnp.float32) + arrived[3].astype(
            jnp.float32
        )

    def last(self):
        self.last_b.wait_recv()
        self.total[self.top] += self.arrived[6].astype(jnp.float32)
        self.last_a.wait_recv()
        self.total[self.low] += self.arrived[7].astype(jnp.float32)

    def drain(self):
        for copy in self.sent:
            copy.wait_send()


def scatter_body(parts_ref, out, near_in, summed, arrived, send_sem, recv_sem):
    scatter = Scatter(parts_ref, near_in, summed, arrived, out, send_sem, recv_sem)
    greet(scatter.peers)
    scatter.begin()
    scatter.early()
    scatter.middle()
    scatter.near()
    scatter.last()
    scatter.drain()


def scatter(parts, collective):
    rows, cols = parts.shape
    rows = rows // 8
    scratch = Scatter.scratch(rows, cols)
    return pl.pallas_call(
        scatter_body,
        in_specs=[pl.BlockSpec(memory_space=pltpu.VMEM)],
        out_specs=pl.BlockSpec(memory_space=pltpu.VMEM),
        out_shape=jax.ShapeDtypeStruct((rows, cols), jnp.float32),
        scratch_shapes=scratch[:3] + scratch[4:],
        compiler_params=pltpu.CompilerParams(collective_id=collective, has_side_effects=True),
        cost_estimate=pl.CostEstimate(flops=0, bytes_accessed=70 * 2**20, transcendentals=0),
        name="scatter",
    )(parts.reshape(8, rows, cols))


BITS = [(i, j, u, v) for i in (0, 1) for j in (0, 1) for u in (0, 1) for v in (0, 1)]
ORDERS = ((0, 2, 1, 3), (2, 0, 3, 1), (1, 3, 0, 2), (3, 1, 2, 0))
PIECE = {(s, j): n for n, (s, j) in enumerate((s, j) for s in range(4) for j in range(-1, s))}


class Trade:
    def __init__(self, source, held, send_sem, recv_sem, peers):
        self.source, self.held = source, held
        self.send_sem, self.recv_sem, self.peers = send_sem, recv_sem, peers
        self.copies = {}
        self.landed = set()

    def land(self, q, s):
        for j in range(-1, s):
            if (q, s, j) not in self.landed:
                self.landed.add((q, s, j))
                self.copies[q, s, j].wait_recv()

    def step(self, q, s):
        order = ORDERS[q]
        for j in range(-1, s):
            pick = [slice(None)] * 4
            pick[order[s]] = 1
            for n in range(j + 1, s):
                pick[order[n]] = 0
            if j < 0:
                source = self.source.at[(*pick, q)]
            else:
                pick[order[j]] = 1
                self.land(q, j)
                source = self.held.at[(q, j, *(p for n, p in enumerate(pick) if n != order[j]))]
            target = self.held.at[(q, s, *(p for n, p in enumerate(pick) if n != order[s]))]
            copy = pltpu.make_async_remote_copy(
                src_ref=source,
                dst_ref=target,
                send_sem=self.send_sem.at[q, PIECE[s, j]],
                recv_sem=self.recv_sem.at[q, PIECE[s, j]],
                device_id={"path": self.peers[order[s]]},
                device_id_type=pl.DeviceIdType.MESH,
            )
            copy.start()
            self.copies[q, s, j] = copy

    def steps(self, s):
        for q in range(4):
            self.step(q, s)

    def finish(self, q):
        for s in range(4):
            self.land(q, s)

    def block(self, q, bits):
        for s in (3, 2, 1, 0):
            if bits[ORDERS[q][s]]:
                return self.held.at[(q, s, *(p for n, p in enumerate(bits) if n != ORDERS[q][s]))]
        return self.source.at[(*bits, q)]

    def drain(self):
        for copy in self.copies.values():
            copy.wait_send()


def trade_body(level, side, *refs):
    share_ref, slot_ref, grad_down, grad_up, mom_down, mom_up = refs[:6]
    refs = refs[6:]
    if side:
        parts_ref, rows_ref, cot_ref, gain_ref = refs[:4]
        refs = refs[4:]
        first_grad = refs[4]
    back_down, back_up, fresh_down, fresh_up = refs[:4]
    refs = refs[5:] if side else refs[4:]
    held, source, moms, outer, send_sem, recv_sem, load_sem, mom_sem, out_sem = refs[:9]
    path = lax.axis_index("path")
    spot_x, spot_z = path // 4, path % 4
    at_x = {(0, 0): spot_x, (1, 0): spot_x + 1 - 2 * (spot_x % 2)}
    at_x.update({(0, 1): 3 - spot_x, (1, 1): (spot_x + 2) % 4})
    at_z = {(0, 0): spot_z, (1, 0): spot_z + 1 - 2 * (spot_z % 2)}
    at_z.update({(0, 1): 3 - spot_z, (1, 1): (spot_z + 2) % 4})
    owner = {k: at_x[k[:2]] * 4 + at_z[k[2:]] for k in BITS}
    peers = [owner[1, 0, 0, 0], owner[0, 1, 0, 0], owner[0, 0, 1, 0], owner[0, 0, 0, 1]]
    loads = []
    for n, grad in enumerate((grad_down, grad_up)):
        loads.append([])
        for k in BITS:
            index = sum(bit << at for at, bit in enumerate(k))
            loads[n].append(
                pltpu.make_async_copy(
                    grad.at[owner[k]], source.at[(n, *k)], load_sem.at[n, index]
                )
            )
            loads[n][-1].start()
    stored = [
        pltpu.make_async_copy(mom, moms.at[n], mom_sem.at[n])
        for n, mom in enumerate((mom_down, mom_up))
    ]
    for copy in stored:
        copy.start()
    barrier = pltpu.get_barrier_semaphore()
    for peer in peers:
        pl.semaphore_signal(
            barrier, inc=1, device_id={"path": peer}, device_id_type=pl.DeviceIdType.MESH
        )
    if side:
        scatter = Scatter(parts_ref, *refs[9:15])
        spread = Spread(first_grad, *refs[15:19])
        for peer in scatter.peers:
            pl.semaphore_signal(
                barrier, inc=1, device_id={"fsdp": peer}, device_id_type=pl.DeviceIdType.MESH
            )
    pl.semaphore_wait(barrier, 7 if side else 4)
    trades = [
        Trade(source.at[n], held.at[n], send_sem.at[n], recv_sem.at[n], peers) for n in range(4)
    ]
    down, up, home_down, home_up = trades
    if side:
        scatter.begin()
    for n in range(2):
        for copy in loads[n]:
            copy.wait()
        trades[n].steps(0)
    hits = {}
    for k in BITS:
        used = share_ref[owner[k], level]
        for m in range(PER_LEVEL):
            hits[k, m] = jnp.where(used == m, 1.0, 0.0).astype(jnp.float32)
    counts = [sum(hits[k, m] for k in BITS) for m in range(PER_LEVEL)]

    def mix(n, q, fresh):
        trades[n].finish(q)

        def rows_of(c, carry):
            rows = pl.ds(pl.multiple_of(c * 16, 16), 16)
            wide = pl.ds(pl.multiple_of(q * 32 + c * 16, 16), 16)
            sums = [jnp.zeros((16, outer.shape[-1]), jnp.float32)] * PER_LEVEL
            for k in BITS:
                part = trades[n].block(q, k)[rows].astype(jnp.float32)
                sums = [total + hits[k, m] * part for m, total in enumerate(sums)]
            for m, total in enumerate(sums):
                divisor = jnp.full((1, total.shape[1]), jnp.maximum(counts[m], 1.0))
                pseudo = total * (1.0 / divisor)
                now = momentum_decay * moms[n, slot_ref[level * PER_LEVEL + m], wide] + pseudo
                fresh[m, wide] = now
                outer[m, rows] = (pseudo + momentum_decay * now).astype(jnp.bfloat16)
            return carry

        lax.fori_loop(0, 2, rows_of, 0)
        for k in BITS:
            source[(n + 2, *k, q)] = outer[share_ref[owner[k], level]]

    def turn(n, fresh):
        for q in range(4):
            mix(n, q, fresh)
            if q:
                trades[n + 2].step(q - 1, 0)
        trades[n + 2].step(3, 0)

    if side:
        scatter.early()
    down.steps(1)
    if side:
        scatter.middle()
    up.steps(1)
    if side:
        scatter.near()
    down.steps(2)
    if side:
        scatter.last()

        def pull(c, carry):
            rows = pl.ds(pl.multiple_of(c * 16, 16), 16)
            value = rows_ref[rows]
            lifted = scatter.total[rows] * gain_ref[...]
            inverse = lax.rsqrt(jnp.mean(value * value, axis=-1, keepdims=True) + epsilon)
            along = jnp.mean(value * lifted, axis=-1, keepdims=True)
            spread.own[rows] = (
                cot_ref[rows].astype(jnp.float32)
                + inverse * lifted
                - value * (inverse * inverse * inverse * along)
            ).astype(jnp.bfloat16)
            return carry

        lax.fori_loop(0, rows_ref.shape[0] // 16, pull, 0)
    up.steps(2)
    if side:
        spread.begin()
    down.steps(3)
    if side:
        spread.relay_first()
    up.steps(3)
    if side:
        spread.relay_second()
    for copy in stored:
        copy.wait()
    turn(0, fresh_down)
    if side:
        spread.relay_last()
    turn(1, fresh_up)
    for s in (1, 2, 3):
        home_down.steps(s)
        home_up.steps(s)
    if side:
        spread.finish()
    for n, out in ((2, back_down), (3, back_up)):
        for q in range(4):
            trades[n].finish(q)
            for k in BITS:
                pltpu.make_async_copy(
                    trades[n].block(q, k), out.at[owner[k], pl.ds(q * 32, 32)], out_sem.at[n - 2]
                ).start()
    for n, out in ((2, back_down), (3, back_up)):
        pltpu.make_async_copy(out, out, out_sem.at[n - 2]).wait()
    for trade in trades:
        trade.drain()
    if side:
        scatter.drain()


def trade(level, share, slots, grad_down, grad_up, mom_down, mom_up, side, collective):
    paths, rows, cols = grad_up.shape
    grad_down, grad_up = (g.reshape(paths, 4, rows // 4, cols) for g in (grad_down, grad_up))
    smem = pl.BlockSpec(memory_space=pltpu.SMEM)
    vmem = pl.BlockSpec(memory_space=pltpu.VMEM)
    hbm = pl.BlockSpec(memory_space=pl.ANY)
    out_shape = [jax.ShapeDtypeStruct((paths, rows, cols), jnp.bfloat16)] * 2
    out_shape += [jax.ShapeDtypeStruct((PER_LEVEL, rows, cols), jnp.float32)] * 2
    out_specs = [hbm, hbm, vmem, vmem]
    scratch = [
        pltpu.VMEM((4, 4, 4, 2, 2, 2, rows // 4, cols), jnp.bfloat16),
        pltpu.VMEM((4, 2, 2, 2, 2, 4, rows // 4, cols), jnp.bfloat16),
        pltpu.VMEM((2, *mom_up.shape), jnp.float32),
        pltpu.VMEM((PER_LEVEL, rows // 4, cols), jnp.bfloat16),
        pltpu.SemaphoreType.DMA((4, 4, 10)),
        pltpu.SemaphoreType.DMA((4, 4, 10)),
        pltpu.SemaphoreType.DMA((2, 16)),
        pltpu.SemaphoreType.DMA((2,)),
        pltpu.SemaphoreType.DMA((2,)),
    ]
    if side:
        tall, wide = side[1].shape
        out_shape += [jax.ShapeDtypeStruct((8, tall, wide), jnp.bfloat16)]
        out_specs += [hbm]
        scratch += Scatter.scratch(tall, wide) + Spread.scratch(tall, wide)
    return pl.pallas_call(
        functools.partial(trade_body, level, bool(side)),
        in_specs=[smem, smem, hbm, hbm, hbm, hbm] + [vmem] * len(side),
        out_specs=out_specs,
        out_shape=out_shape,
        scratch_shapes=scratch,
        compiler_params=pltpu.CompilerParams(
            collective_id=collective, has_side_effects=True, vmem_limit_bytes=60 * 2**20
        ),
        cost_estimate=pl.CostEstimate(flops=0, bytes_accessed=300 * 2**20, transcendentals=0),
        name="trade",
    )(share, slots, grad_down, grad_up, mom_down, mom_up, *side)


def shards(
    tokens, cotangent, norm_gain, up_proj, down_proj, mom_up, mom_down, share_table, module_slot
):
    scale_in = 1.0 / math.sqrt(2048)
    scale_out = 1.0 / math.sqrt(4096)
    norm_gains = norm_gain[0]
    up_local = up_proj[0]
    down_local = down_proj[0]
    paths = share_table.shape[0]
    row_block, col_block = mom_up.shape[1:]

    def blocks(grad):
        return grad.astype(jnp.bfloat16).reshape(paths, row_block, col_block)

    cot_all = lax.all_gather(cotangent[0], "fsdp", axis=0, tiled=True)
    tok_float = tokens[0].astype(jnp.float32)
    first_normed = gather(rms_norm(tok_float, norm_gains[0]).astype(jnp.bfloat16), 0)
    first_pre = jnp.dot(first_normed, up_local[0], preferred_element_type=jnp.float32) * scale_in
    first_hidden = gelu_tanh(first_pre).astype(jnp.bfloat16)
    second_input = tok_float + scatter(
        (contract_last(first_hidden, down_local[0]) * scale_out).astype(jnp.bfloat16), 1
    )
    second_normed = gather(rms_norm(second_input, norm_gains[1]).astype(jnp.bfloat16), 2)
    second_pre = jnp.dot(second_normed, up_local[1], preferred_element_type=jnp.float32) * scale_in
    second_hidden = gelu_tanh(second_pre).astype(jnp.bfloat16)
    grad_down_upper = contract_first(cot_all, second_hidden) * scale_out
    second_slope = (
        jnp.dot(cot_all, down_local[1], preferred_element_type=jnp.float32)
        * scale_out
        * gelu_slope(second_pre)
    ).astype(jnp.bfloat16)
    grad_up_upper = contract_first(second_normed, second_slope) * scale_in
    back_parts = (contract_last(second_slope, up_local[1]) * scale_in).astype(jnp.bfloat16)
    tall, wide = tok_float.shape
    back_down, back_up, fresh_down, fresh_up, first_grad = trade(
        1,
        share_table,
        module_slot,
        blocks(grad_down_upper),
        blocks(grad_up_upper),
        mom_down,
        mom_up,
        (
            back_parts.reshape(8, tall, wide),
            second_input,
            cotangent[0],
            norm_gains[1].reshape(1, wide),
        ),
        3,
    )
    first_grad = first_grad.reshape(8 * tall, wide)
    down_1 = update(1, down_proj, back_down, ())
    up_1 = update(1, up_proj, back_up, ())
    mom_down_1 = place(1, module_slot, fresh_down, mom_down.shape[0], ())
    mom_up_1 = place(1, module_slot, fresh_up, mom_up.shape[0], ())
    grad_down_lower = contract_first(first_grad, first_hidden) * scale_out
    first_slope = (
        jnp.dot(first_grad, down_local[0], preferred_element_type=jnp.float32)
        * scale_out
        * gelu_slope(first_pre)
    ).astype(jnp.bfloat16)
    grad_up_lower = contract_first(first_normed, first_slope) * scale_in
    back_down, back_up, fresh_down, fresh_up = trade(
        0,
        share_table,
        module_slot,
        blocks(grad_down_lower),
        blocks(grad_up_lower),
        mom_down,
        mom_up,
        (),
        4,
    )
    new_down = update(0, down_proj, back_down, (down_1,))
    new_up = update(0, up_proj, back_up, (up_1,))
    new_mom_down = place(0, module_slot, fresh_down, mom_down.shape[0], (mom_down_1,))
    new_mom_up = place(0, module_slot, fresh_up, mom_up.shape[0], (mom_up_1,))
    return (new_up, new_down, new_mom_up, new_mom_down)


def solution(mesh):
    in_specs = (
        P("path", "fsdp", None),
        P("path", "fsdp", None),
        P("path", None, None),
        P("path", None, None, "fsdp"),
        P("path", None, None, "fsdp"),
        P(None, "path", "fsdp"),
        P(None, "path", "fsdp"),
        P(),
        P(),
    )
    out_specs = (
        P("path", None, None, "fsdp"),
        P("path", None, None, "fsdp"),
        P(None, "path", "fsdp"),
        P(None, "path", "fsdp"),
    )
    return jax.shard_map(shards, mesh=mesh, in_specs=in_specs, out_specs=out_specs, check_vma=False)
```

```python
import functools
import math

import jax
import jax.numpy as jnp
from jax import lax
from jax.experimental import pallas as pl
from jax.experimental.pallas import tpu as pltpu
from jax.sharding import PartitionSpec as P

PER_LEVEL = 4

epsilon = 1e-06
gelu_coef = 0.7978845608
cubic_coef = 0.044715
momentum_decay = 0.9
outer_rate = 0.7


def gelu_tanh(value):
    inner = gelu_coef * (value + cubic_coef * value * value * value)
    return 0.5 * value * (1.0 + jnp.tanh(inner))


def gelu_slope(value):
    inner = gelu_coef * (value + cubic_coef * value * value * value)
    tangent = jnp.tanh(inner)
    return 0.5 * (1.0 + tangent) + 0.5 * value * (1.0 - tangent * tangent) * gelu_coef * (
        1.0 + 3.0 * cubic_coef * value * value
    )


def rms_norm(rows, gain):
    return rows * lax.rsqrt(jnp.mean(rows * rows, axis=-1, keepdims=True) + epsilon) * gain


def norm_back(rows, gain, upstream):
    _, pull = jax.vjp(lambda inner_rows: rms_norm(inner_rows, gain), rows)
    return pull(upstream)[0]


def contract_last(left, right):
    return lax.dot_general(
        left, right, (((1,), (1,)), ((), ())), preferred_element_type=jnp.float32
    )


def contract_first(left, right):
    return lax.dot_general(
        left, right, (((0,), (0,)), ((), ())), preferred_element_type=jnp.float32
    )


def update_body(up, down, *refs):
    backs, news = refs[:4], refs[4:]
    for n, (old, new) in enumerate(((up, news[0]), (down, news[1]))):
        for level in range(2):
            new[0, level] = (
                old[0, level].astype(jnp.float32)
                - outer_rate * backs[2 * n + level][...].astype(jnp.float32)
            ).astype(jnp.bfloat16)


def update(up, down, backs):
    _, levels, rows, cols = up.shape
    step = 256
    full = pl.BlockSpec((1, levels, step, cols), lambda r: (0, 0, r, 0))
    flat = pl.BlockSpec((step, cols), lambda r: (r, 0))
    return pl.pallas_call(
        update_body,
        grid=(rows // step,),
        in_specs=[full, full] + [flat] * 4,
        out_specs=[full, full],
        out_shape=[jax.ShapeDtypeStruct(up.shape, up.dtype)] * 2,
        name="update",
    )(up, down, *(back.reshape(rows, cols) for back in backs))


def cube():
    place = lax.axis_index("fsdp")
    row, core = place // 2, place % 2
    across = row + 1 - 2 * (row % 2)
    return row, core, across, 3 - row, (row + 2) % 4


def greet(peers):
    barrier = pltpu.get_barrier_semaphore()
    for peer in peers:
        pl.semaphore_signal(
            barrier, inc=1, device_id={"fsdp": peer}, device_id_type=pl.DeviceIdType.MESH
        )
    pl.semaphore_wait(barrier, len(peers))


class Spread:
    @staticmethod
    def scratch(rows, cols):
        sems = pltpu.SemaphoreType.DMA((13,))
        return [pltpu.VMEM((rows, cols), jnp.bfloat16), sems, sems, pltpu.SemaphoreType.DMA]

    def __init__(self, out, own, send_sem, recv_sem, local_sem):
        self.out, self.own = out, own
        self.send_sem, self.recv_sem, self.local_sem = send_sem, recv_sem, local_sem
        row, core, row_a, row_b, row_d = cube()
        self.me, self.sibling = row * 2 + core, row * 2 + 1 - core
        self.peer_a, self.peer_b = row_a * 2 + core, row_b * 2 + core
        self.block_d = row_d * 2 + core
        self.peers = (self.sibling, self.peer_a, self.peer_b)
        half = own.shape[0] // 2
        self.first, self.second = pl.ds(0, half), pl.ds(half, half)
        self.side, self.sent, self.done = [], [], set()

    def got(self, copy):
        if id(copy) not in self.done:
            self.done.add(id(copy))
            copy.wait_recv()

    def near_blocks(self):
        self.stay.wait()
        self.got(self.mine)
        return self.me, self.sibling

    def own_blocks(self):
        return self.peer_a, self.peer_b

    def other_blocks(self):
        for copy in self.side[:4]:
            self.got(copy)
        turn = self.sibling - self.me
        return self.peer_a + turn, self.peer_b + turn

    def far_blocks(self):
        for copy in self.side[4:]:
            self.got(copy)
        return self.block_d, self.block_d + self.sibling - self.me

    def copy(self, index, source, target, peer):
        copy = pltpu.make_async_remote_copy(
            src_ref=source,
            dst_ref=target,
            send_sem=self.send_sem.at[index],
            recv_sem=self.recv_sem.at[index],
            device_id={"fsdp": peer},
            device_id_type=pl.DeviceIdType.MESH,
        )
        copy.start()
        self.sent.append(copy)
        return copy

    def relay(self, index, block, part, peer):
        place = self.out.at[block, part]
        return self.copy(index, place, place, peer)

    def begin(self):
        own, out, me, first, second = self.own, self.out, self.me, self.first, self.second
        self.a_second = self.copy(0, own.at[second], out.at[me, second], self.peer_a)
        self.b_first = self.copy(1, own.at[first], out.at[me, first], self.peer_b)
        self.a_first = self.copy(2, own.at[first], out.at[me, first], self.peer_a)
        self.b_second = self.copy(3, own.at[second], out.at[me, second], self.peer_b)
        self.mine = self.copy(4, own, out.at[me], self.sibling)
        self.stay = pltpu.make_async_copy(own, out.at[me], self.local_sem)
        self.stay.start()

    def relay_first(self):
        self.got(self.b_first)
        self.onward_a = self.relay(5, self.peer_b, self.first, self.peer_a)
        self.got(self.a_second)
        self.onward_b = self.relay(6, self.peer_a, self.second, self.peer_b)
        self.side.append(self.relay(7, self.peer_b, self.first, self.sibling))
        self.side.append(self.relay(8, self.peer_a, self.second, self.sibling))

    def relay_second(self):
        self.got(self.a_first)
        self.side.append(self.relay(9, self.peer_a, self.first, self.sibling))
        self.got(self.b_second)
        self.side.append(self.relay(10, self.peer_b, self.second, self.sibling))

    def relay_last(self):
        self.got(self.onward_a)
        self.side.append(self.relay(11, self.block_d, self.first, self.sibling))
        self.got(self.onward_b)
        self.side.append(self.relay(12, self.block_d, self.second, self.sibling))

    def finish(self):
        for copy in (self.mine, *self.side):
            self.got(copy)
        for copy in self.sent:
            copy.wait_send()


class Scatter:
    @staticmethod
    def scratch(rows, cols):
        sems = pltpu.SemaphoreType.DMA((10,))
        pair = pltpu.VMEM((4, rows, cols), jnp.bfloat16)
        return [
            pair,
            pair,
            pltpu.VMEM((8, rows // 2, cols), jnp.bfloat16),
            pltpu.VMEM((rows, cols), jnp.float32),
            sems,
            sems,
        ]

    def __init__(self, parts_ref, near_in, summed, arrived, total, send_sem, recv_sem):
        self.parts, self.near_in, self.summed = parts_ref, near_in, summed
        self.arrived, self.total = arrived, total
        self.send_sem, self.recv_sem = send_sem, recv_sem
        row, self.core, row_a, row_b, row_d = cube()
        self.sibling = row * 2 + 1 - self.core
        self.peer_a, self.peer_b = row_a * 2 + self.core, row_b * 2 + self.core
        self.peers = (self.sibling, self.peer_a, self.peer_b)
        half = total.shape[0] // 2
        self.top, self.low = pl.ds(0, half), pl.ds(half, half)
        self.order = (row_d, row_a, row_b, row)
        self.sent, self.swaps = [], {}

    def copy(self, index, source, target, peer):
        copy = pltpu.make_async_remote_copy(
            src_ref=source,
            dst_ref=target,
            send_sem=self.send_sem.at[index],
            recv_sem=self.recv_sem.at[index],
            device_id={"fsdp": peer},
            device_id_type=pl.DeviceIdType.MESH,
        )
        copy.start()
        self.sent.append(copy)
        return copy

    def swap(self, k):
        self.swaps[k] = self.copy(
            k,
            self.parts.at[self.order[k] * 2 + 1 - self.core],
            self.near_in.at[k],
            self.sibling,
        )

    def settle(self, k):
        self.swaps[k].wait_recv()
        mine = self.parts[self.order[k] * 2 + self.core].astype(jnp.float32)
        self.summed[k] = (mine + self.near_in[k].astype(jnp.float32)).astype(jnp.bfloat16)

    def send_far(self):
        self.far_a = self.copy(
            4, self.summed.at[0, self.top], self.arrived.at[0], self.peer_a
        )
        self.far_b = self.copy(
            5, self.summed.at[0, self.low], self.arrived.at[1], self.peer_b
        )

    def send_near_a(self):
        self.near_a = self.copy(
            6, self.summed.at[1, self.top], self.arrived.at[2], self.peer_a
        )

    def send_near_b(self):
        self.near_b = self.copy(
            7, self.summed.at[2, self.low], self.arrived.at[3], self.peer_b
        )

    def begin(self):
        for k in range(4):
            self.swap(k)

    def early(self):
        self.settle(0)
        self.settle(1)
        self.send_far()
        self.settle(2)
        self.send_near_a()
        self.settle(3)
        self.send_near_b()

    def middle(self):
        summed, arrived = self.summed, self.arrived
        self.far_a.wait_recv()
        arrived[4] = (
            summed[2, self.top].astype(jnp.float32) + arrived[0].astype(jnp.float32)
        ).astype(jnp.bfloat16)
        self.far_b.wait_recv()
        arrived[5] = (
            summed[1, self.low].astype(jnp.float32) + arrived[1].astype(jnp.float32)
        ).astype(jnp.bfloat16)
        self.last_b = self.copy(8, arrived.at[4], arrived.at[6], self.peer_b)
        self.last_a = self.copy(9, arrived.at[5], arrived.at[7], self.peer_a)

    def near(self):
        summed, arrived = self.summed, self.arrived
        self.near_a.wait_recv()
        self.total[self.top] = summed[3, self.top].astype(jnp.float32) + arrived[2].astype(
            jnp.float32
        )
        self.near_b.wait_recv()
        self.total[self.low] = summed[3, self.low].astype(jnp.float32) + arrived[3].astype(
            jnp.float32
        )

    def last(self):
        self.last_b.wait_recv()
        self.total[self.top] += self.arrived[6].astype(jnp.float32)
        self.last_a.wait_recv()
        self.total[self.low] += self.arrived[7].astype(jnp.float32)

    def drain(self):
        for copy in self.sent:
            copy.wait_send()


def normalise(rows_ref, gain, out):
    def chunk(c, carry):
        rows = pl.ds(pl.multiple_of(c * 16, 16), 16)
        value = rows_ref[rows].astype(jnp.float32)
        inverse = lax.rsqrt(jnp.mean(value * value, axis=-1, keepdims=True) + epsilon)
        out[rows] = (value * inverse * gain).astype(jnp.bfloat16)
        return carry

    lax.fori_loop(0, rows_ref.shape[0] // 16, chunk, 0)


def front_body(scale_in, scale_out, *refs):
    tok, cot, gain, up_hbm, down_hbm = refs[:5]
    normed_out, pre_out, hidden_out, input_out, second_out, second_pre_out, cot_out = refs[5:12]
    up_first, up_second, down_first, normed, second, pre, hidden, second_pre, parts = refs[12:21]
    refs = refs[21:]
    scatter = Scatter(parts, *refs[:6])
    tokens = Spread(normed, *refs[6:10])
    later = Spread(second, *refs[10:14])
    upstream = Spread(cot_out, cot, *refs[14:17])
    load_sem, normed_sem, second_sem, out_sem = refs[17:21]
    loads = [
        pltpu.make_async_copy(source, target, load_sem.at[n])
        for n, (source, target) in enumerate(
            (
                (up_hbm.at[0, 0], up_first),
                (down_hbm.at[0, 0], down_first),
                (up_hbm.at[0, 1], up_second),
            )
        )
    ]
    for copy in loads:
        copy.start()
    normalise(tok, gain[0, pl.ds(0, 1)], tokens.own)
    greet(scatter.peers)
    tokens.begin()
    leaving = []

    def leave(source, target, sem):
        leaving.append(pltpu.make_async_copy(source, target, sem))
        leaving[-1].start()

    def lower(pair):
        first, other = pair

        def one(n, carry):
            block = first + n * (other - first)
            value = scale_in * jnp.dot(
                normed[block], up_first[...], preferred_element_type=jnp.float32
            )
            pre[block] = value
            active = gelu_tanh(value).astype(jnp.bfloat16)
            hidden[block] = active
            parts[block] = (contract_last(active, down_first[...]) * scale_out).astype(
                jnp.bfloat16
            )
            return carry

        lax.fori_loop(0, 2, one, 0)
        for block in pair:
            leave(normed.at[block], normed_out.at[block], normed_sem.at[len(leaving)])

    def upper(pair):
        first, other = pair

        def one(n, carry):
            block = first + n * (other - first)
            second_pre[block] = scale_in * jnp.dot(
                second[block], up_second[...], preferred_element_type=jnp.float32
            )
            return carry

        lax.fori_loop(0, 2, one, 0)
        for block in pair:
            leave(second.at[block], second_out.at[block], second_sem.at[len(leaving) - 11])

    loads[0].wait()
    loads[1].wait()
    lower(tokens.near_blocks())
    tokens.relay_first()
    tokens.relay_second()
    lower(tokens.own_blocks())
    lower(tokens.other_blocks())
    scatter.swap(1)
    scatter.swap(2)
    scatter.swap(3)
    tokens.relay_last()
    scatter.settle(1)
    scatter.send_near_a()
    scatter.settle(2)
    scatter.send_near_b()
    lower(tokens.far_blocks())
    scatter.swap(0)
    scatter.settle(3)
    scatter.settle(0)
    scatter.send_far()
    leave(pre, pre_out, out_sem.at[0])
    leave(hidden, hidden_out, out_sem.at[1])
    scatter.middle()
    upstream.begin()
    scatter.near()
    scatter.last()
    total = scatter.total

    def settle(c, carry):
        rows = pl.ds(pl.multiple_of(c * 16, 16), 16)
        total[rows] += tok[rows].astype(jnp.float32)
        return carry

    lax.fori_loop(0, tok.shape[0] // 16, settle, 0)
    normalise(total, gain[0, pl.ds(1, 1)], later.own)
    leave(total, input_out, out_sem.at[2])
    upstream.relay_first()
    later.begin()
    upstream.relay_second()
    loads[2].wait()
    upper(later.near_blocks())
    later.relay_first()
    upstream.relay_last()
    later.relay_second()
    upper(later.own_blocks())
    upper(later.other_blocks())
    later.relay_last()
    upper(later.far_blocks())
    leave(second_pre, second_pre_out, out_sem.at[3])
    upstream.stay.wait()
    for spread in (tokens, upstream, later):
        spread.finish()
    scatter.drain()
    for copy in leaving:
        copy.wait()


def front(tok, cot, gain, up, down, scale_in, scale_out, collective):
    rows, wide = tok.shape
    cols = up.shape[-1]
    vmem = pl.BlockSpec(memory_space=pltpu.VMEM)
    hbm = pl.BlockSpec(memory_space=pl.ANY)
    narrow, full = (8, rows, cols), (8, rows, wide)
    outs = [
        (full, jnp.bfloat16),
        (narrow, jnp.float32),
        (narrow, jnp.bfloat16),
        ((rows, wide), jnp.float32),
        (full, jnp.bfloat16),
        (narrow, jnp.float32),
        (full, jnp.bfloat16),
    ]
    weight = pltpu.VMEM((wide, cols), jnp.bfloat16)
    tall = pltpu.VMEM(full, jnp.bfloat16)
    wait = pltpu.SemaphoreType.DMA
    return pl.pallas_call(
        functools.partial(front_body, scale_in, scale_out),
        in_specs=[vmem, vmem, vmem, hbm, hbm],
        out_specs=[hbm] * 7,
        out_shape=[jax.ShapeDtypeStruct(shape, kind) for shape, kind in outs],
        scratch_shapes=[
            weight,
            weight,
            weight,
            tall,
            tall,
            pltpu.VMEM(narrow, jnp.float32),
            pltpu.VMEM(narrow, jnp.bfloat16),
            pltpu.VMEM(narrow, jnp.float32),
            tall,
            *Scatter.scratch(rows, wide),
            *Spread.scratch(rows, wide),
            *Spread.scratch(rows, wide),
            *Spread.scratch(rows, wide)[1:],
            wait((3,)),
            wait((8,)),
            wait((8,)),
            wait((4,)),
        ],
        compiler_params=pltpu.CompilerParams(
            collective_id=collective, has_side_effects=True, vmem_limit_bytes=60 * 2**20
        ),
        name="front",
    )(tok, cot, gain, up, down)


BITS = [(i, j, u, v) for i in (0, 1) for j in (0, 1) for u in (0, 1) for v in (0, 1)]
ORDERS = ((0, 2, 1, 3), (2, 0, 3, 1), (1, 3, 0, 2), (3, 1, 2, 0))
PIECE = {(s, j): n for n, (s, j) in enumerate((s, j) for s in range(4) for j in range(-1, s))}


class Trade:
    def __init__(self, source, held, send_sem, recv_sem, peers):
        self.source, self.held = source, held
        self.send_sem, self.recv_sem, self.peers = send_sem, recv_sem, peers
        self.copies = {}
        self.landed = set()

    def land(self, q, s):
        for j in range(-1, s):
            if (q, s, j) not in self.landed:
                self.landed.add((q, s, j))
                self.copies[q, s, j].wait_recv()

    def step(self, q, s):
        order = ORDERS[q]
        for j in range(-1, s):
            pick = [slice(None)] * 4
            pick[order[s]] = 1
            for n in range(j + 1, s):
                pick[order[n]] = 0
            if j < 0:
                source = self.source.at[(*pick, q)]
            else:
                pick[order[j]] = 1
                self.land(q, j)
                source = self.held.at[(q, j, *(p for n, p in enumerate(pick) if n != order[j]))]
            target = self.held.at[(q, s, *(p for n, p in enumerate(pick) if n != order[s]))]
            copy = pltpu.make_async_remote_copy(
                src_ref=source,
                dst_ref=target,
                send_sem=self.send_sem.at[q, PIECE[s, j]],
                recv_sem=self.recv_sem.at[q, PIECE[s, j]],
                device_id={"path": self.peers[order[s]]},
                device_id_type=pl.DeviceIdType.MESH,
            )
            copy.start()
            self.copies[q, s, j] = copy

    def steps(self, s):
        for q in range(4):
            self.step(q, s)

    def finish(self, q):
        for s in range(4):
            self.land(q, s)

    def block(self, q, bits):
        for s in (3, 2, 1, 0):
            if bits[ORDERS[q][s]]:
                return self.held.at[(q, s, *(p for n, p in enumerate(bits) if n != ORDERS[q][s]))]
        return self.source.at[(*bits, q)]

    def drain(self):
        for copy in self.copies.values():
            copy.wait_send()


def trade_body(level, side, *refs):
    share_ref, slot_ref, grad_down, grad_up, mom_down, mom_up = refs[:6]
    refs = refs[6:]
    if not side:
        other_down, other_up = refs[:2]
        refs = refs[2:]
    if side:
        parts_ref, rows_ref, cot_ref, gain_ref = refs[:4]
        refs = refs[4:]
        first_grad = refs[4]
    back_down, back_up, fresh_down, fresh_up = refs[:4]
    refs = refs[5:] if side else refs[4:]
    if not side:
        module_mom, mom_out_sem = refs[9:11]
    held, source, moms, outer, send_sem, recv_sem, load_sem, mom_sem, out_sem = refs[:9]
    path = lax.axis_index("path")
    spot_x, spot_z = path // 4, path % 4
    at_x = {(0, 0): spot_x, (1, 0): spot_x + 1 - 2 * (spot_x % 2)}
    at_x.update({(0, 1): 3 - spot_x, (1, 1): (spot_x + 2) % 4})
    at_z = {(0, 0): spot_z, (1, 0): spot_z + 1 - 2 * (spot_z % 2)}
    at_z.update({(0, 1): 3 - spot_z, (1, 1): (spot_z + 2) % 4})
    owner = {k: at_x[k[:2]] * 4 + at_z[k[2:]] for k in BITS}
    peers = [owner[1, 0, 0, 0], owner[0, 1, 0, 0], owner[0, 0, 1, 0], owner[0, 0, 0, 1]]
    loads = []
    for n, grad in enumerate((grad_down, grad_up)):
        loads.append([])
        for k in BITS:
            index = sum(bit << at for at, bit in enumerate(k))
            loads[n].append(
                pltpu.make_async_copy(
                    grad.at[owner[k]], source.at[(n, *k)], load_sem.at[n, index]
                )
            )
            loads[n][-1].start()
    stored = [
        pltpu.make_async_copy(mom, moms.at[n], mom_sem.at[n])
        for n, mom in enumerate((mom_down, mom_up))
    ]
    if not side:
        stored += [
            pltpu.make_async_copy(other, module_mom.at[n, 1], mom_sem.at[2 + n])
            for n, other in enumerate((other_down, other_up))
        ]
    for copy in stored:
        copy.start()
    barrier = pltpu.get_barrier_semaphore()
    for peer in peers:
        pl.semaphore_signal(
            barrier, inc=1, device_id={"path": peer}, device_id_type=pl.DeviceIdType.MESH
        )
    if side:
        scatter = Scatter(parts_ref, *refs[9:15])
        spread = Spread(first_grad, *refs[15:19])
        for peer in scatter.peers:
            pl.semaphore_signal(
                barrier, inc=1, device_id={"fsdp": peer}, device_id_type=pl.DeviceIdType.MESH
            )
    pl.semaphore_wait(barrier, 7 if side else 4)
    trades = [
        Trade(source.at[n], held.at[n], send_sem.at[n], recv_sem.at[n], peers) for n in range(4)
    ]
    down, up, home_down, home_up = trades
    if side:
        scatter.begin()
    for n in range(2):
        for copy in loads[n]:
            copy.wait()
        trades[n].steps(0)
    hits = {}
    for k in BITS:
        used = share_ref[owner[k], level]
        for m in range(PER_LEVEL):
            hits[k, m] = jnp.where(used == m, 1.0, 0.0).astype(jnp.float32)
    counts = [sum(hits[k, m] for k in BITS) for m in range(PER_LEVEL)]

    def mix(n, q, fresh):
        trades[n].finish(q)

        def rows_of(c, carry):
            rows = pl.ds(pl.multiple_of(c * 16, 16), 16)
            wide = pl.ds(pl.multiple_of(q * 32 + c * 16, 16), 16)
            sums = [jnp.zeros((16, outer.shape[-1]), jnp.float32)] * PER_LEVEL
            for k in BITS:
                part = trades[n].block(q, k)[rows].astype(jnp.float32)
                sums = [total + hits[k, m] * part for m, total in enumerate(sums)]
            for m, total in enumerate(sums):
                divisor = jnp.full((1, total.shape[1]), jnp.maximum(counts[m], 1.0))
                pseudo = total * (1.0 / divisor)
                now = momentum_decay * moms[n, slot_ref[level * PER_LEVEL + m], wide] + pseudo
                fresh[m, wide] = now
                outer[m, rows] = (pseudo + momentum_decay * now).astype(jnp.bfloat16)
            return carry

        lax.fori_loop(0, 2, rows_of, 0)
        for k in BITS:
            source[(n + 2, *k, q)] = outer[share_ref[owner[k], level]]

    def turn(n, fresh):
        for q in range(4):
            mix(n, q, fresh)
            if q:
                trades[n + 2].step(q - 1, 0)
        trades[n + 2].step(3, 0)

    def settle(n, out):
        for slot in range(mom_up.shape[0]):
            module = jnp.int32(0)
            for m in range(1, 2 * PER_LEVEL):
                module = jnp.where(slot_ref[m] == slot, m, module)
            moms[n, slot] = module_mom[n, module // PER_LEVEL, module % PER_LEVEL]
        pltpu.make_async_copy(moms.at[n], out, mom_out_sem.at[n]).start()

    if side:
        scatter.early()
    down.steps(1)
    if side:
        scatter.middle()
    up.steps(1)
    if side:
        scatter.near()
    down.steps(2)
    if side:
        scatter.last()

        def pull(c, carry):
            rows = pl.ds(pl.multiple_of(c * 16, 16), 16)
            value = rows_ref[rows]
            lifted = scatter.total[rows] * gain_ref[...]
            inverse = lax.rsqrt(jnp.mean(value * value, axis=-1, keepdims=True) + epsilon)
            along = jnp.mean(value * lifted, axis=-1, keepdims=True)
            spread.own[rows] = (
                cot_ref[rows].astype(jnp.float32)
                + inverse * lifted
                - value * (inverse * inverse * inverse * along)
            ).astype(jnp.bfloat16)
            return carry

        lax.fori_loop(0, rows_ref.shape[0] // 16, pull, 0)
    up.steps(2)
    if side:
        spread.begin()
    down.steps(3)
    if side:
        spread.relay_first()
    up.steps(3)
    if side:
        spread.relay_second()
    for copy in stored:
        copy.wait()
    turn(0, fresh_down if side else module_mom.at[0, 0])
    if side:
        spread.relay_last()
    turn(1, fresh_up if side else module_mom.at[1, 0])
    home_down.steps(1)
    if not side:
        settle(0, fresh_down)
    home_up.steps(1)
    if not side:
        settle(1, fresh_up)
    for s in (2, 3):
        home_down.steps(s)
        home_up.steps(s)
    if side:
        spread.stay.wait()
        spread.finish()
    else:
        for n, out in enumerate((fresh_down, fresh_up)):
            pltpu.make_async_copy(moms.at[n], out, mom_out_sem.at[n]).wait()
    for n, out in ((2, back_down), (3, back_up)):
        for q in range(4):
            trades[n].finish(q)
            for k in BITS:
                pltpu.make_async_copy(
                    trades[n].block(q, k), out.at[owner[k], pl.ds(q * 32, 32)], out_sem.at[n - 2]
                ).start()
    for n, out in ((2, back_down), (3, back_up)):
        pltpu.make_async_copy(out, out, out_sem.at[n - 2]).wait()
    for trade in trades:
        trade.drain()
    if side:
        scatter.drain()


def trade(level, share, slots, grad_down, grad_up, mom_down, mom_up, side, other, collective):
    paths, rows, cols = grad_up.shape
    grad_down, grad_up = (g.reshape(paths, 4, rows // 4, cols) for g in (grad_down, grad_up))
    smem = pl.BlockSpec(memory_space=pltpu.SMEM)
    vmem = pl.BlockSpec(memory_space=pltpu.VMEM)
    hbm = pl.BlockSpec(memory_space=pl.ANY)
    out_shape = [jax.ShapeDtypeStruct((paths, rows, cols), jnp.bfloat16)] * 2
    fresh = (PER_LEVEL, rows, cols) if side else mom_up.shape
    out_shape += [jax.ShapeDtypeStruct(fresh, jnp.float32)] * 2
    out_specs = [hbm, hbm] + [vmem if side else hbm] * 2
    scratch = [
        pltpu.VMEM((4, 4, 4, 2, 2, 2, rows // 4, cols), jnp.bfloat16),
        pltpu.VMEM((4, 2, 2, 2, 2, 4, rows // 4, cols), jnp.bfloat16),
        pltpu.VMEM((2, *mom_up.shape), jnp.float32),
        pltpu.VMEM((PER_LEVEL, rows // 4, cols), jnp.bfloat16),
        pltpu.SemaphoreType.DMA((4, 4, 10)),
        pltpu.SemaphoreType.DMA((4, 4, 10)),
        pltpu.SemaphoreType.DMA((2, 16)),
        pltpu.SemaphoreType.DMA((4,)),
        pltpu.SemaphoreType.DMA((2,)),
    ]
    if not side:
        scratch += [
            pltpu.VMEM((2, 2, PER_LEVEL, rows, cols), jnp.float32),
            pltpu.SemaphoreType.DMA((2,)),
        ]
    if side:
        tall, wide = side[1].shape
        out_shape += [jax.ShapeDtypeStruct((8, tall, wide), jnp.bfloat16)]
        out_specs += [hbm]
        scratch += Scatter.scratch(tall, wide) + Spread.scratch(tall, wide)
    return pl.pallas_call(
        functools.partial(trade_body, level, bool(side)),
        in_specs=[smem, smem, hbm, hbm, hbm, hbm] + [hbm] * len(other) + [vmem] * len(side),
        out_specs=out_specs,
        out_shape=out_shape,
        scratch_shapes=scratch,
        compiler_params=pltpu.CompilerParams(
            collective_id=collective, has_side_effects=True, vmem_limit_bytes=60 * 2**20
        ),
        cost_estimate=pl.CostEstimate(flops=0, bytes_accessed=300 * 2**20, transcendentals=0),
        name="trade",
    )(share, slots, grad_down, grad_up, mom_down, mom_up, *other, *side)


def shards(
    tokens, cotangent, norm_gain, up_proj, down_proj, mom_up, mom_down, share_table, module_slot
):
    scale_in = 1.0 / math.sqrt(2048)
    scale_out = 1.0 / math.sqrt(4096)
    norm_gains = norm_gain[0]
    up_local = up_proj[0]
    down_local = down_proj[0]
    paths = share_table.shape[0]
    row_block, col_block = mom_up.shape[1:]

    def blocks(grad):
        return grad.astype(jnp.bfloat16).reshape(paths, row_block, col_block)

    outs = front(
        tokens[0], cotangent[0], norm_gain, up_proj, down_proj, scale_in, scale_out, 0
    )
    tall, wide = tokens.shape[1:]
    second_input = outs[3]
    first_normed, first_pre, first_hidden, second_normed, second_pre, cot_all = (
        outs[n].reshape(8 * tall, -1) for n in (0, 1, 2, 4, 5, 6)
    )
    second_hidden = gelu_tanh(second_pre).astype(jnp.bfloat16)
    grad_down_upper = contract_first(cot_all, second_hidden) * scale_out
    second_slope = (
        jnp.dot(cot_all, down_local[1], preferred_element_type=jnp.float32)
        * scale_out
        * gelu_slope(second_pre)
    ).astype(jnp.bfloat16)
    grad_up_upper = contract_first(second_normed, second_slope) * scale_in
    back_parts = (contract_last(second_slope, up_local[1]) * scale_in).astype(jnp.bfloat16)
    back_down_1, back_up_1, fresh_down, fresh_up, first_grad = trade(
        1,
        share_table,
        module_slot,
        blocks(grad_down_upper),
        blocks(grad_up_upper),
        mom_down,
        mom_up,
        (
            back_parts.reshape(8, tall, wide),
            second_input,
            cotangent[0],
            norm_gains[1].reshape(1, wide),
        ),
        (),
        3,
    )
    first_grad = first_grad.reshape(8 * tall, wide)
    grad_down_lower = contract_first(first_grad, first_hidden) * scale_out
    first_slope = (
        jnp.dot(first_grad, down_local[0], preferred_element_type=jnp.float32)
        * scale_out
        * gelu_slope(first_pre)
    ).astype(jnp.bfloat16)
    grad_up_lower = contract_first(first_normed, first_slope) * scale_in
    back_down_0, back_up_0, new_mom_down, new_mom_up = trade(
        0,
        share_table,
        module_slot,
        blocks(grad_down_lower),
        blocks(grad_up_lower),
        mom_down,
        mom_up,
        (),
        (fresh_down, fresh_up),
        4,
    )
    new_up, new_down = update(
        up_proj, down_proj, (back_up_0, back_up_1, back_down_0, back_down_1)
    )
    return (new_up, new_down, new_mom_up, new_mom_down)


def solution(mesh):
    in_specs = (
        P("path", "fsdp", None),
        P("path", "fsdp", None),
        P("path", None, None),
        P("path", None, None, "fsdp"),
        P("path", None, None, "fsdp"),
        P(None, "path", "fsdp"),
        P(None, "path", "fsdp"),
        P(),
        P(),
    )
    out_specs = (
        P("path", None, None, "fsdp"),
        P("path", None, None, "fsdp"),
        P(None, "path", "fsdp"),
        P(None, "path", "fsdp"),
    )
    return jax.shard_map(shards, mesh=mesh, in_specs=in_specs, out_specs=out_specs, check_vma=False)
```
